32 devices in a mesh: dp: 2 (over core), row: 4 (over z), col: 4 (over y, x).
Axes of the slice: x: 2, y: 2, z: 4, core: 2. Of those that a mesh axis runs over, the one named last changes fastest.
Arguments:
- inputs: bfloat16 [4096, 2048], P(('dp', 'row'), 'col'), may hold values from -20 to 20
- segment: int32 [8, 512], P(('dp', 'col')), may hold values from 0 to 15, as said below
- grad_output: bfloat16 [4096, 2048], P(('dp', 'row'), 'col'), may hold values from -6 to 6
- norm_gain: float32 [2048], P('col'), may hold values from 0.1 to 1.9
- norm_bias: float32 [2048], P('col'), may hold values from -3 to 3
- qkv_weight: bfloat16 [2048, 6144], P('col', 'row'), may hold values from -4 to 4
- qkv_bias: float32 [6144], P('row'), may hold values from -3 to 3
- dense_weight: bfloat16 [2048, 2048], P('row', 'col'), may hold values from -0.5 to 0.5
- dense_bias: float32 [2048], P('col'), may hold values from -2 to 2
- fc1_weight: bfloat16 [2048, 8192], P('col', 'row'), may hold values from -0.125 to 0.125
- fc1_bias: float32 [8192], P('row'), may hold values from -3 to 3
- fc2_weight: bfloat16 [8192, 2048], P('row', 'col'), may hold values from -0.09375 to 0.09375
- fc2_bias: float32 [2048], P('col'), may hold values from -2 to 2
Outputs:
- output: bfloat16 [4096, 2048], P(('dp', 'row'), 'col')
- grad_input: float32 [4096, 2048], P(('dp', 'row'), 'col')
- grad_norm_gain: float32 [2048], P('col')
- grad_norm_bias: float32 [2048], P('col')
- grad_qkv_weight: float32 [2048, 6144], P('col', 'row')
- grad_qkv_bias: float32 [6144], P('row')
- grad_dense_weight: float32 [2048, 2048], P('row', 'col')
- grad_dense_bias: float32 [2048], P('col')
- grad_fc1_weight: float32 [2048, 8192], P('col', 'row')
- grad_fc1_bias: float32 [8192], P('row')
- grad_fc2_weight: float32 [8192, 2048], P('row', 'col')
- grad_fc2_bias: float32 [2048], P('col')
The draws below stay inside these ranges and needn't reach their ends.
Inputs may be any that keep to these rules, and one draw needn't show every extreme that they name: `segment`: in each row of 512 tokens the ids start at 0 and never fall; a run of equal ids is one sequence. Rows 0, 4, 8 and so on hold one sequence of 512 tokens; rows 3, 7, 11 and so on hold 16 sequences of 32 tokens.
All inputs are finite; a program needn't handle non-finite values.
Results may differ from the reference program's by a relative error of at most 0.0098.
Values may be sent and summed in bfloat16 or wider, within the bound.
No kernel may reach another device: no remote copies, remote signals or barrier semaphores. Data moves between devices by JAX's collectives and lax.ppermute only.
A program may use at most 192 MiB of HBM per device.

```python
import math
import jax
import jax.numpy as jnp
from jax import lax

HEADS = 32
HEAD_DIM = 64
ROT = 32
FF = 8192
PACK = 512
D = 2048
TOKENS = 4096
N_COL = 4


def draw_inputs(key, part):
    noise_key, col_key, row_key = jax.random.split(key, 3)
    ramp = jnp.arange(D, dtype=jnp.float32) / D
    columns = 0.2 * jnp.exp(math.log(10.0) * ramp + jax.random.uniform(col_key, (D,), jnp.float32, -0.3, 0.3))
    rows = jnp.exp(jax.random.uniform(row_key, (TOKENS, 1), jnp.float32, -0.6, 0.6))
    noise = jnp.clip(jax.random.normal(noise_key, (TOKENS, D), jnp.float32), -4.0, 4.0)
    return (rows * noise * columns).astype(jnp.bfloat16)


def draw_qkv_weight(key, part):
    base = jnp.clip(jax.random.normal(key, (D, HEADS, 3, HEAD_DIM), jnp.float32), -6.0, 6.0) / math.sqrt(D)
    return base.reshape(D, 3 * D).astype(jnp.bfloat16)


def draw_segment(key, part):
    count = TOKENS // PACK
    places = jnp.arange(PACK)
    row_ids = jnp.arange(count)
    cuts = jax.random.randint(key, (count, PACK), 0, 40) == 0
    drawn = ((row_ids % 4 != 0) & (row_ids % 4 != 3))[:, None]
    cuts = cuts & (places[None, :] > 0) & drawn
    even = (row_ids % 4 == 3)[:, None] & (places[None, :] % (PACK // 16) == 0) & (places[None, :] > 0)
    cuts = cuts | even
    ids = jnp.cumsum(cuts.astype(jnp.int32), axis=1)
    return jnp.minimum(ids, 15).astype(jnp.int32)


def level_of(own_key, extent, pieces, least, high):
    gain, own = 1.0, jax.random.fold_in(own_key, 6)
    for dim, shards_of in pieces:
        steps = jnp.exp(jax.random.uniform(jax.random.fold_in(own, dim), (shards_of,), jnp.float32, least / len(pieces), high / len(pieces)))
        gain = gain * jnp.repeat(steps, extent[dim] // shards_of).reshape([-1 if axis == dim else 1 for axis in range(len(extent))])
    return gain


def normal_values(stream_key, shape, scale, limit, cuts=(), held_as=jnp.bfloat16):
    level = level_of(stream_key, shape, cuts, -0.22, 0.18) if cuts else 1.0
    result = jax.random.normal(stream_key, shape, jnp.float32) * scale * level
    return jnp.minimum(jnp.maximum(result, -limit), limit).astype(held_as)


def setup_inputs(seed: int = 0) -> dict:
    key_of = jax.random.split(jax.random.key(seed), 14)
    return {
        "inputs": draw_inputs(jax.random.fold_in(key_of[13], 71), 0),
        "segment": draw_segment(jax.random.fold_in(key_of[13], 71), 0),
        "grad_output": normal_values(key_of[2], (TOKENS, D), 1.0, 6.0, ((0, 8), (1, 4))),
        "norm_gain": jnp.clip(1.0 + 0.18 * jax.random.normal(key_of[3], (D,), jnp.float32), 0.1, 1.9),
        "norm_bias": normal_values(key_of[4], (D,), 0.5, 3.0, ((0, 4),), jnp.float32),
        "qkv_weight": draw_qkv_weight(jax.random.fold_in(key_of[13], 71), 0),
        "qkv_bias": normal_values(key_of[6], (3 * D,), 0.5, 3.0, ((0, 4),), jnp.float32),
        "dense_weight": normal_values(key_of[7], (D, D), (D // 16) ** -0.5, 0.5, ((0, 4), (1, 4))),
        "dense_bias": normal_values(key_of[8], (D,), 0.3, 2.0, ((0, 4),), jnp.float32),
        "fc1_weight": normal_values(key_of[9], (D, FF), D ** -0.5, 0.125, ((0, 4), (1, 4))),
        "fc1_bias": normal_values(key_of[10], (FF,), 0.5, 3.0, ((0, 4),), jnp.float32),
        "fc2_weight": normal_values(key_of[11], (FF, D), (FF // 2) ** -0.5, 0.09375, ((0, 4), (1, 4))),
        "fc2_bias": normal_values(key_of[12], (D,), 0.3, 2.0, ((0, 4),), jnp.float32),
    }


EPS = 1e-05

def gelu_tanh(values):
    inner = 0.7978845608028654 * (values + 0.044715 * values * values * values)
    return 0.5 * values * (1.0 + jnp.tanh(inner))

def gelu_slope(values):
    inner = 0.7978845608028654 * (values + 0.044715 * values * values * values)
    tangent = jnp.tanh(inner)
    return 0.5 * (1.0 + tangent) + 0.5 * values * (1.0 - tangent * tangent) * 0.7978845608028654 * (1.0 + 0.134145 * values * values)

def rotary_tables(segment, rot_dims):
    width = segment.shape[1]
    places = jnp.arange(width, dtype=jnp.int32)
    fresh = jnp.concatenate([jnp.ones((segment.shape[0], 1), dtype=jnp.bool_), segment[:, 1:] != segment[:, :-1]], axis=1)
    starts = lax.cummax(jnp.where(fresh, places[None, :], jnp.zeros_like(segment)), axis=1)
    offsets = (places[None, :] - starts).astype(jnp.float32)
    half_rot = rot_dims // 2
    freqs = jnp.exp(jnp.arange(half_rot, dtype=jnp.float32) * (-2.0 * math.log(10000.0) / rot_dims))
    angles = offsets[:, :, None] * freqs
    return (jnp.cos(angles)[:, :, None, :], jnp.sin(angles)[:, :, None, :])

def rotate_forward(values, cosines, sines, rot_dims):
    half_rot = rot_dims // 2
    first = values[..., :half_rot]
    second = values[..., half_rot:rot_dims]
    return jnp.concatenate([first * cosines - second * sines, second * cosines + first * sines, values[..., rot_dims:]], axis=-1)

def rotate_back(grads, cosines, sines, rot_dims):
    half_rot = rot_dims // 2
    first = grads[..., :half_rot]
    second = grads[..., half_rot:rot_dims]
    return jnp.concatenate([first * cosines + second * sines, second * cosines - first * sines, grads[..., rot_dims:]], axis=-1)

def masked_scores(query, key_rows, segment_row):
    places = jnp.arange(segment_row.shape[0], dtype=jnp.int32)
    allowed = (segment_row[:, None] == segment_row[None, :]) & (places[None, :] <= places[:, None])
    scale = query.shape[-1] ** (-0.5)
    scores = jnp.einsum('qhe,khe->hqk', query.astype(jnp.float32), key_rows.astype(jnp.float32)) * scale
    return (jnp.where(allowed[None, :, :], scores, -1e+30), scale)

def pack_forward(items):
    query, key_rows, value, segment_row = items
    scores, scale = masked_scores(query, key_rows, segment_row)
    row_top = lax.optimization_barrier(jnp.max(scores, axis=-1, keepdims=True))
    log_total = row_top[..., 0] + jnp.log(lax.optimization_barrier(jnp.sum(jnp.exp(scores - row_top), axis=-1)))
    chances = jnp.exp(scores - log_total[..., None]).astype(jnp.bfloat16)
    attended = jnp.einsum('hqk,khe->qhe', chances.astype(jnp.float32), value.astype(jnp.float32)).astype(jnp.bfloat16)
    return (attended, log_total)

def pack_backward(items):
    query, key_rows, value, attended, grad_att, log_total, segment_row = items
    scores, scale = masked_scores(query, key_rows, segment_row)
    chances = jnp.exp(scores - log_total[..., None])
    rounded = chances.astype(jnp.bfloat16)
    grad_wide = grad_att.astype(jnp.float32)
    grad_value = jnp.einsum('hqk,qhe->khe', rounded.astype(jnp.float32), grad_wide)
    grad_chance = jnp.einsum('qhe,khe->hqk', grad_wide, value.astype(jnp.float32))
    delta = jnp.transpose(lax.optimization_barrier(jnp.sum(grad_wide * attended.astype(jnp.float32), axis=-1)))
    grad_scores = (chances * (grad_chance - delta[:, :, None]) * scale).astype(jnp.bfloat16)
    grad_query = jnp.einsum('hqk,khe->qhe', grad_scores.astype(jnp.float32), key_rows.astype(jnp.float32))
    grad_key = jnp.einsum('hqk,qhe->khe', grad_scores.astype(jnp.float32), query.astype(jnp.float32))
    return (grad_query, grad_key, grad_value)

def reference(inputs, segment, grad_output, norm_gain, norm_bias, qkv_weight, qkv_bias, dense_weight, dense_bias, fc1_weight, fc1_bias, fc2_weight, fc2_bias):
    block_rows = N_COL * PACK
    block_count = TOKENS // block_rows
    packs_block = block_rows // PACK

    def one_block(carry, items):
        block_in, block_grad, block_seg = items
        wide_in = block_in.astype(jnp.float32)
        row_mean = lax.optimization_barrier(jnp.mean(wide_in, axis=1, keepdims=True))
        row_square = lax.optimization_barrier(jnp.mean(wide_in * wide_in, axis=1, keepdims=True))
        inv_std = lax.rsqrt(row_square - row_mean * row_mean + EPS)
        centered = (wide_in - row_mean) * inv_std
        normed = (centered * norm_gain + norm_bias).astype(jnp.bfloat16)
        qkv_full = jnp.dot(normed, qkv_weight, preferred_element_type=jnp.float32) + qkv_bias
        pre_act = jnp.dot(normed, fc1_weight, preferred_element_type=jnp.float32) + fc1_bias
        hidden = gelu_tanh(pre_act).astype(jnp.bfloat16)
        split_qkv = qkv_full.reshape(packs_block, PACK, HEADS, 3, HEAD_DIM)
        cosines, sines = rotary_tables(block_seg, ROT)
        query = rotate_forward(split_qkv[:, :, :, 0, :], cosines, sines, ROT).astype(jnp.bfloat16)
        key_rows = rotate_forward(split_qkv[:, :, :, 1, :], cosines, sines, ROT).astype(jnp.bfloat16)
        value = split_qkv[:, :, :, 2, :].astype(jnp.bfloat16)
        attended, log_total = lax.map(pack_forward, (query, key_rows, value, block_seg))
        att_flat = attended.reshape(block_rows, D)
        mixed = jnp.dot(att_flat, dense_weight, preferred_element_type=jnp.float32) + dense_bias + (jnp.dot(hidden, fc2_weight, preferred_element_type=jnp.float32) + fc2_bias)
        block_out = (wide_in + mixed).astype(jnp.bfloat16)
        grad_dense_w = jnp.dot(att_flat.T, block_grad, preferred_element_type=jnp.float32)
        grad_fc2_w = jnp.dot(hidden.T, block_grad, preferred_element_type=jnp.float32)
        grad_out_b = lax.optimization_barrier(jnp.sum(block_grad.astype(jnp.float32), axis=0))
        grad_att = jnp.dot(block_grad, dense_weight.T, preferred_element_type=jnp.float32).astype(jnp.bfloat16)
        grad_hidden = jnp.dot(block_grad, fc2_weight.T, preferred_element_type=jnp.float32)
        grad_pre = (grad_hidden * gelu_slope(pre_act)).astype(jnp.bfloat16)
        grad_query, grad_key, grad_value = lax.map(pack_backward, (query, key_rows, value, attended, grad_att.reshape(packs_block, PACK, HEADS, HEAD_DIM), log_total, block_seg))
        grad_query = rotate_back(grad_query, cosines, sines, ROT)
        grad_key = rotate_back(grad_key, cosines, sines, ROT)
        grad_qkv = jnp.stack([grad_query, grad_key, grad_value], axis=3).reshape(block_rows, 3 * D).astype(jnp.bfloat16)
        grad_qkv_w = jnp.dot(normed.T, grad_qkv, preferred_element_type=jnp.float32)
        grad_qkv_b = lax.optimization_barrier(jnp.sum(grad_qkv.astype(jnp.float32), axis=0))
        grad_fc1_w = jnp.dot(normed.T, grad_pre, preferred_element_type=jnp.float32)
        grad_fc1_b = lax.optimization_barrier(jnp.sum(grad_pre.astype(jnp.float32), axis=0))
        grad_normed = jnp.dot(grad_qkv, qkv_weight.T, preferred_element_type=jnp.float32) + jnp.dot(grad_pre, fc1_weight.T, preferred_element_type=jnp.float32)
        grad_gain = lax.optimization_barrier(jnp.sum(grad_normed * centered, axis=0))
        grad_bias = lax.optimization_barrier(jnp.sum(grad_normed, axis=0))
        scaled = grad_normed * norm_gain
        grad_in = block_grad.astype(jnp.float32) + inv_std * (scaled - lax.optimization_barrier(jnp.mean(scaled, axis=1, keepdims=True)) - centered * lax.optimization_barrier(jnp.mean(scaled * centered, axis=1, keepdims=True)))
        update = (grad_gain, grad_bias, grad_qkv_w, grad_qkv_b, grad_dense_w, grad_out_b, grad_fc1_w, grad_fc1_b, grad_fc2_w)
        new_carry = jax.tree.map(lambda left, right: left + right, carry, update)
        return (new_carry, (block_out, grad_in))
    start = (jnp.zeros((D,), jnp.float32), jnp.zeros((D,), jnp.float32), jnp.zeros((D, 3 * D), jnp.float32), jnp.zeros((3 * D,), jnp.float32), jnp.zeros((D, D), jnp.float32), jnp.zeros((D,), jnp.float32), jnp.zeros((D, FF), jnp.float32), jnp.zeros((FF,), jnp.float32), jnp.zeros((FF, D), jnp.float32))
    sums, stacked = lax.scan(one_block, start, (inputs.reshape(block_count, block_rows, D), grad_output.reshape(block_count, block_rows, D), segment.reshape(block_count, packs_block, PACK)))
    grad_gain, grad_bias, grad_qkv_w, grad_qkv_b, grad_dense_w, grad_out_b, grad_fc1_w, grad_fc1_b, grad_fc2_w = sums
    output = stacked[0].reshape(TOKENS, D)
    grad_input = stacked[1].reshape(TOKENS, D)
    return (output, grad_input, grad_gain, grad_bias, grad_qkv_w, grad_qkv_b, grad_dense_w, grad_out_b, grad_fc1_w, grad_fc1_b, grad_fc2_w, grad_out_b)
```

```python
import math

import jax
import jax.numpy as jnp
from jax import lax
from jax.sharding import PartitionSpec as P

HEAD_DIM = 64
ROT = 32
PACK = 512


EPS = 1e-05


def gelu_tanh(values):
    inner = 0.7978845608028654 * (values + 0.044715 * values * values * values)
    return 0.5 * values * (1.0 + jnp.tanh(inner))


def gelu_slope(values):
    inner = 0.7978845608028654 * (values + 0.044715 * values * values * values)
    tangent = jnp.tanh(inner)
    return 0.5 * (1.0 + tangent) + 0.5 * values * (1.0 - tangent * tangent) * 0.7978845608028654 * (
        1.0 + 0.134145 * values * values
    )


def rotary_tables(segment, rot_dims):
    width = segment.shape[1]
    places = jnp.arange(width, dtype=jnp.int32)
    fresh = jnp.concatenate(
        [jnp.ones((segment.shape[0], 1), dtype=jnp.bool_), segment[:, 1:] != segment[:, :-1]],
        axis=1,
    )
    starts = lax.cummax(jnp.where(fresh, places[None, :], jnp.zeros_like(segment)), axis=1)
    offsets = (places[None, :] - starts).astype(jnp.float32)
    half_rot = rot_dims // 2
    freqs = jnp.exp(jnp.arange(half_rot, dtype=jnp.float32) * (-2.0 * math.log(10000.0) / rot_dims))
    angles = offsets[:, :, None] * freqs
    return (jnp.cos(angles)[:, :, None, :], jnp.sin(angles)[:, :, None, :])


def rotate_forward(values, cosines, sines, rot_dims):
    half_rot = rot_dims // 2
    first = values[..., :half_rot]
    second = values[..., half_rot:rot_dims]
    return jnp.concatenate(
        [
            first * cosines - second * sines,
            second * cosines + first * sines,
            values[..., rot_dims:],
        ],
        axis=-1,
    )


def rotate_back(grads, cosines, sines, rot_dims):
    half_rot = rot_dims // 2
    first = grads[..., :half_rot]
    second = grads[..., half_rot:rot_dims]
    return jnp.concatenate(
        [first * cosines + second * sines, second * cosines - first * sines, grads[..., rot_dims:]],
        axis=-1,
    )


def masked_scores(query, key_rows, segment_row):
    places = jnp.arange(segment_row.shape[0], dtype=jnp.int32)
    allowed = (segment_row[:, None] == segment_row[None, :]) & (places[None, :] <= places[:, None])
    scale = query.shape[-1] ** (-0.5)
    scores = jnp.einsum("qhe,khe->hqk", query, key_rows, preferred_element_type=jnp.float32) * scale
    return (jnp.where(allowed[None, :, :], scores, -1e30), scale)


def pack_forward(items):
    query, key_rows, value, segment_row = items
    scores, scale = masked_scores(query, key_rows, segment_row)
    row_top = jnp.max(scores, axis=-1, keepdims=True)
    log_total = row_top[..., 0] + jnp.log(jnp.sum(jnp.exp(scores - row_top), axis=-1))
    chances = jnp.exp(scores - log_total[..., None]).astype(jnp.bfloat16)
    attended = jnp.einsum(
        "hqk,khe->qhe", chances, value, preferred_element_type=jnp.float32
    ).astype(jnp.bfloat16)
    return (attended, log_total)


def pack_backward(items):
    query, key_rows, value, attended, grad_att, log_total, segment_row = items
    scores, scale = masked_scores(query, key_rows, segment_row)
    chances = jnp.exp(scores - log_total[..., None])
    rounded = chances.astype(jnp.bfloat16)
    grad_value = jnp.einsum("hqk,qhe->khe", rounded, grad_att, preferred_element_type=jnp.float32)
    grad_chance = jnp.einsum("qhe,khe->hqk", grad_att, value, preferred_element_type=jnp.float32)
    delta = jnp.transpose(
        jnp.sum(grad_att.astype(jnp.float32) * attended.astype(jnp.float32), axis=-1)
    )
    grad_scores = (chances * (grad_chance - delta[:, :, None]) * scale).astype(jnp.bfloat16)
    grad_query = jnp.einsum(
        "hqk,khe->qhe", grad_scores, key_rows, preferred_element_type=jnp.float32
    )
    grad_key = jnp.einsum("hqk,qhe->khe", grad_scores, query, preferred_element_type=jnp.float32)
    return (grad_query, grad_key, grad_value)


def contract_rows(left, right):
    return lax.dot_general(
        left, right, (((0,), (0,)), ((), ())), preferred_element_type=jnp.float32
    )


def col_partner(step, n_col):
    if n_col & (n_col - 1) == 0:
        return [(i, i ^ step) for i in range(n_col)]
    return [(i, (step - i) % n_col) for i in range(n_col)]


def partner_of(index, step, n_col):
    if n_col & (n_col - 1) == 0:
        return index ^ step
    return (step - index) % n_col


def line_gather(block, axis):
    count = lax.axis_size(axis)
    here = lax.axis_index(axis)
    stacked = jnp.zeros((count,) + block.shape, block.dtype)
    ups = [block]
    downs = [block]
    for step in range(count - 1):
        ups.append(lax.ppermute(ups[-1], axis, [(i, i + 1) for i in range(step, count - 1)]))
        downs.append(
            lax.ppermute(downs[-1], axis, [(i + 1, i) for i in range(0, count - 1 - step)])
        )
    zero = (0,) * block.ndim
    stacked = lax.dynamic_update_slice(stacked, block[None], (here,) + zero)
    for step in range(1, count):
        piece = jnp.where(here >= step, ups[step], downs[count - step])
        stacked = lax.dynamic_update_slice(stacked, piece[None], ((here - step) % count,) + zero)
    return stacked


def line_scatter(blocks, axis):
    count = lax.axis_size(axis)
    here = lax.axis_index(axis)

    def pick(index):
        return lax.dynamic_index_in_dim(blocks, jnp.clip(index, 0, count - 1), 0, keepdims=False)

    up = None
    down = None
    for step in range(count - 1):
        send_up = pick(here + count - 1 - step)
        send_down = pick(here - (count - 1) + step)
        if step:
            send_up = add_wide(send_up, up)
            send_down = add_wide(send_down, down)
        up = lax.ppermute(send_up, axis, [(i, i + 1) for i in range(0, step + 1)])
        down = lax.ppermute(
            send_down, axis, [(i + 1, i) for i in range(count - 2 - step, count - 1)]
        )
    total = pick(here).astype(jnp.float32)
    if count > 1:
        total = total + up.astype(jnp.float32) + down.astype(jnp.float32)
    return total


def add_wide(left, right):
    return (left.astype(jnp.float32) + right.astype(jnp.float32)).astype(left.dtype)


def shifts(axis, step):
    count = lax.axis_size(axis)
    return [((i + step) % count, i) for i in range(count)]


def spread_tokens(block):
    n_col = lax.axis_size("col")
    col = lax.axis_index("col")
    n_dp = lax.axis_size("dp")
    rows = line_gather(block, "row")
    width = block.shape[1]
    groups = rows.reshape(n_col, -1, width)
    own = lax.dynamic_index_in_dim(groups, col, 0, keepdims=False)
    wide = jnp.zeros((own.shape[0], n_col * width), block.dtype)
    got = [(col, own)]
    start = 1 if n_col & (n_col - 1) == 0 else 0
    for step in range(start, n_col):
        other = partner_of(col, step, n_col)
        sent = lax.dynamic_index_in_dim(groups, other, 0, keepdims=False)
        got.append((other, lax.ppermute(sent, "col", col_partner(step, n_col))))
    for index, piece in got:
        wide = lax.dynamic_update_slice(wide, piece, (0, index * width))
    return jnp.stack([wide] + [lax.ppermute(wide, "dp", shifts("dp", s)) for s in range(1, n_dp)])


def collect_tokens(partial):
    n_col = lax.axis_size("col")
    col = lax.axis_index("col")
    n_dp = lax.axis_size("dp")
    n_row = lax.axis_size("row")
    summed = partial[:, 0]
    for s in range(1, n_dp):
        summed = add_wide(summed, lax.ppermute(partial[:, s], "dp", shifts("dp", n_dp - s)))
    own = lax.dynamic_index_in_dim(summed, col, 0, keepdims=False)
    groups = jnp.zeros_like(summed)
    got = [(col, own)]
    start = 1 if n_col & (n_col - 1) == 0 else 0
    for step in range(start, n_col):
        other = partner_of(col, step, n_col)
        sent = lax.dynamic_index_in_dim(summed, other, 0, keepdims=False)
        got.append((other, lax.ppermute(sent, "col", col_partner(step, n_col))))
    for index, piece in got:
        groups = lax.dynamic_update_slice(groups, piece[None], (index, 0, 0))
    return line_scatter(groups.reshape(n_row, -1, groups.shape[-1]), "row")


def half_of(array, axis):
    size = array.shape[axis] // lax.axis_size("dp")
    return lax.dynamic_slice_in_dim(array, lax.axis_index("dp") * size, size, axis)


def both_halves(own, axis):
    n_dp = lax.axis_size("dp")
    here = lax.axis_index("dp")
    parts = [own] + [lax.ppermute(own, "dp", shifts("dp", s)) for s in range(1, n_dp)]
    if n_dp == 2:
        return jnp.where(
            here == 0,
            jnp.concatenate(parts, axis=axis),
            jnp.concatenate(parts[::-1], axis=axis),
        )
    size = own.shape[axis]
    out = jnp.concatenate(parts, axis=axis)
    for s in range(n_dp):
        out = lax.dynamic_update_slice_in_dim(out, parts[s], ((here + s) % n_dp) * size, axis)
    return out


def body(
    inputs,
    segment,
    grad_output,
    norm_gain,
    norm_bias,
    qkv_weight,
    qkv_bias,
    dense_weight,
    dense_bias,
    fc1_weight,
    fc1_bias,
    fc2_weight,
    fc2_bias,
):
    n_col = lax.axis_size("col")
    n_dp = lax.axis_size("dp")
    width = inputs.shape[1]
    in_half = jnp.concatenate([half_of(qkv_weight, 1), half_of(fc1_weight, 1)], axis=1)
    back_half = jnp.concatenate([half_of(dense_weight, 0), half_of(fc2_weight, 0)], axis=0)
    qkv_cols = qkv_weight.shape[1] // n_dp
    att_cols = dense_weight.shape[0] // n_dp
    back_all = lax.all_gather(back_half, "col", axis=0)
    in_all = lax.all_gather(in_half, "col", axis=0, tiled=True)

    grad_rows = spread_tokens(grad_output)
    tokens = grad_rows.shape[0] * grad_rows.shape[1]
    grad_rows = grad_rows.reshape(tokens, n_col, width)

    wide_in = inputs.astype(jnp.float32)
    row_total, row_squares = lax.psum(
        (jnp.sum(wide_in, axis=1), jnp.sum(wide_in * wide_in, axis=1)), "col"
    )
    full_width = n_col * width
    row_mean = (row_total / full_width)[:, None]
    row_square = (row_squares / full_width)[:, None]
    inv_std = lax.rsqrt(row_square - row_mean * row_mean + EPS)
    centered = (wide_in - row_mean) * inv_std
    normed = (centered * norm_gain + norm_bias).astype(jnp.bfloat16)
    normed_rows = spread_tokens(normed).reshape(tokens, full_width)
    seg_rows = jnp.concatenate(
        [segment] + [lax.ppermute(segment, "dp", shifts("dp", s)) for s in range(1, n_dp)]
    )

    backed = jnp.einsum(
        "tjk,jhk->th", grad_rows, back_all, preferred_element_type=jnp.float32
    )
    grad_att = backed[:, :att_cols].astype(jnp.bfloat16)

    projected = jnp.dot(normed_rows, in_all, preferred_element_type=jnp.float32)
    qkv_full = projected[:, :qkv_cols] + half_of(qkv_bias, 0)
    pre_act = projected[:, qkv_cols:] + half_of(fc1_bias, 0)
    hidden = gelu_tanh(pre_act).astype(jnp.bfloat16)
    grad_pre = (backed[:, att_cols:] * gelu_slope(pre_act)).astype(jnp.bfloat16)

    def grads_back(left):
        part = jnp.einsum(
            "th,tjk->jhk", left, grad_rows, preferred_element_type=jnp.float32
        ).astype(jnp.bfloat16)
        return lax.psum_scatter(part, "col", scatter_dimension=0, tiled=False)

    def grads_in(right):
        part = contract_rows(normed_rows, right).astype(jnp.bfloat16)
        return lax.psum_scatter(part, "col", scatter_dimension=0, tiled=True)

    grad_fc2_half = grads_back(hidden)
    grad_fc1_half = grads_in(grad_pre)

    packs_here = seg_rows.shape[0]
    heads_here = qkv_cols // (3 * HEAD_DIM)
    split_qkv = qkv_full.reshape(packs_here, PACK, heads_here, 3, HEAD_DIM)
    cosines, sines = rotary_tables(seg_rows, ROT)
    query = rotate_forward(split_qkv[:, :, :, 0, :], cosines, sines, ROT).astype(jnp.bfloat16)
    key_rows = rotate_forward(split_qkv[:, :, :, 1, :], cosines, sines, ROT).astype(jnp.bfloat16)
    value = split_qkv[:, :, :, 2, :].astype(jnp.bfloat16)
    attended, log_total = lax.map(pack_forward, (query, key_rows, value, seg_rows))
    att_flat = attended.reshape(tokens, att_cols)

    acts = jnp.concatenate([att_flat, hidden], axis=1)
    out_part = jnp.einsum(
        "th,jhk->jtk", acts, back_all, preferred_element_type=jnp.float32
    ).astype(jnp.bfloat16)
    mixed = collect_tokens(out_part.reshape(n_col, n_dp, tokens // n_dp, width))
    output = (wide_in + (mixed + dense_bias + fc2_bias)).astype(jnp.bfloat16)

    grad_query, grad_key, grad_value = lax.map(
        pack_backward,
        (
            query,
            key_rows,
            value,
            attended,
            grad_att.reshape(packs_here, PACK, heads_here, HEAD_DIM),
            log_total,
            seg_rows,
        ),
    )
    grad_query = rotate_back(grad_query, cosines, sines, ROT)
    grad_key = rotate_back(grad_key, cosines, sines, ROT)
    grad_qkv = (
        jnp.stack([grad_query, grad_key, grad_value], axis=3)
        .reshape(tokens, qkv_cols)
        .astype(jnp.bfloat16)
    )
    grad_first = jnp.concatenate([grad_qkv, grad_pre], axis=1)
    norm_part = jnp.einsum(
        "tf,jkf->jtk",
        grad_first,
        in_all.reshape(n_col, width, -1),
        preferred_element_type=jnp.float32,
    ).astype(jnp.bfloat16)
    grad_normed = collect_tokens(norm_part.reshape(n_col, n_dp, tokens // n_dp, width))
    grad_dense_half = grads_back(att_flat)
    grad_qkv_half = grads_in(grad_qkv)
    grad_in_b = lax.psum(jnp.sum(grad_first.astype(jnp.float32), axis=0), "col")

    scaled = grad_normed * norm_gain
    scaled_sum, cross_sum = lax.psum(
        (jnp.sum(scaled, axis=1), jnp.sum(scaled * centered, axis=1)), "col"
    )
    grad_wide = grad_output.astype(jnp.float32)
    grad_input = grad_wide + inv_std * (
        scaled - (scaled_sum / full_width)[:, None] - centered * (cross_sum / full_width)[:, None]
    )
    grad_gain, grad_bias, grad_out_b = lax.psum(
        (
            jnp.sum(grad_normed * centered, axis=0),
            jnp.sum(grad_normed, axis=0),
            jnp.sum(grad_wide, axis=0),
        ),
        ("dp", "row"),
    )
    return (
        output,
        grad_input,
        grad_gain,
        grad_bias,
        both_halves(grad_qkv_half, 1).astype(jnp.float32),
        both_halves(grad_in_b[:qkv_cols], 0),
        both_halves(grad_dense_half, 0).astype(jnp.float32),
        grad_out_b,
        both_halves(grad_fc1_half, 1).astype(jnp.float32),
        both_halves(grad_in_b[qkv_cols:], 0),
        both_halves(grad_fc2_half, 0).astype(jnp.float32),
        grad_out_b,
    )


def solution(mesh):
    in_specs = (
        P(("dp", "row"), "col"),
        P(("dp", "col"), None),
        P(("dp", "row"), "col"),
        P("col"),
        P("col"),
        P("col", "row"),
        P("row"),
        P("row", "col"),
        P("col"),
        P("col", "row"),
        P("row"),
        P("row", "col"),
        P("col"),
    )
    out_specs = (
        P(("dp", "row"), "col"),
        P(("dp", "row"), "col"),
        P("col"),
        P("col"),
        P("col", "row"),
        P("row"),
        P("row", "col"),
        P("col"),
        P("col", "row"),
        P("row"),
        P("row", "col"),
        P("col"),
    )
    return jax.shard_map(body, mesh=mesh, in_specs=in_specs, out_specs=out_specs, check_vma=False)
```

```python
import math

import jax
import jax.numpy as jnp
from jax import lax
from jax.experimental import pallas as pl
from jax.experimental.pallas import tpu as pltpu
from jax.sharding import PartitionSpec as P

HEAD_DIM = 64
ROT = 32
PACK = 512


EPS = 1e-05


def gelu_tanh(values):
    inner = 0.7978845608028654 * (values + 0.044715 * values * values * values)
    return 0.5 * values * (1.0 + jnp.tanh(inner))


def gelu_slope(values):
    inner = 0.7978845608028654 * (values + 0.044715 * values * values * values)
    tangent = jnp.tanh(inner)
    return 0.5 * (1.0 + tangent) + 0.5 * values * (1.0 - tangent * tangent) * 0.7978845608028654 * (
        1.0 + 0.134145 * values * values
    )


def rotary_tables(segment, columns):
    width = segment.shape[1]
    places = jnp.arange(width, dtype=jnp.int32)
    fresh = jnp.concatenate(
        [jnp.ones((segment.shape[0], 1), dtype=jnp.bool_), segment[:, 1:] != segment[:, :-1]],
        axis=1,
    )
    starts = lax.cummax(jnp.where(fresh, places[None, :], jnp.zeros_like(segment)), axis=1)
    offsets = (places[None, :] - starts).astype(jnp.float32).reshape(-1, 1)
    half_rot = ROT // 2
    column = jnp.arange(3 * HEAD_DIM, dtype=jnp.int32)
    part = column % HEAD_DIM
    turned = (column < 2 * HEAD_DIM) & (part < ROT)
    freqs = jnp.exp((part % half_rot).astype(jnp.float32) * (-2.0 * math.log(10000.0) / ROT))
    freqs = jnp.where(turned, freqs, 0.0)
    sign = jnp.where(turned, jnp.where(part < half_rot, -1.0, 1.0), 0.0)
    angles = offsets * freqs[None, :]
    repeats = columns // (3 * HEAD_DIM)
    cosines = jnp.concatenate([jnp.cos(angles)] * repeats, axis=1)
    sines = jnp.concatenate([jnp.sin(angles) * sign[None, :]] * repeats, axis=1)
    return cosines, sines


def dot_nt(left, right):
    return lax.dot_general(
        left, right, (((1,), (1,)), ((), ())), preferred_element_type=jnp.float32
    )


def dot_tn(left, right):
    return lax.dot_general(
        left, right, (((0,), (0,)), ((), ())), preferred_element_type=jnp.float32
    )


def dot_nn(left, right):
    return jnp.dot(left, right, preferred_element_type=jnp.float32)


def attention_kernel(
    qkv_ref, bias_ref, cos_ref, sin_ref, seg_col_ref, seg_row_ref, grad_ref, out_ref, back_ref, turned, grads
):
    heads = out_ref.shape[1] // HEAD_DIM
    columns = qkv_ref.shape[1]
    half_rot = ROT // 2
    lanes = lax.broadcasted_iota(jnp.int32, (1, columns), 1) % HEAD_DIM
    first = lanes < half_rot

    def partner(values):
        ahead = pltpu.roll(values, columns - half_rot, 1)
        behind = pltpu.roll(values, half_rot, 1)
        return jnp.where(first, ahead, behind)

    full = qkv_ref[...] + bias_ref[...]
    turned[...] = (full * cos_ref[...] + partner(full) * sin_ref[...]).astype(jnp.bfloat16)
    size = qkv_ref.shape[0]
    rows = lax.broadcasted_iota(jnp.int32, (size, size), 0)
    places = lax.broadcasted_iota(jnp.int32, (size, size), 1)
    allowed = (seg_col_ref[0] == seg_row_ref[0]) & (places <= rows)
    scale = HEAD_DIM ** (-0.5)
    for head in range(heads):
        base = head * 3 * HEAD_DIM
        own = slice(head * HEAD_DIM, (head + 1) * HEAD_DIM)
        query = turned[:, base : base + HEAD_DIM]
        key = turned[:, base + HEAD_DIM : base + 2 * HEAD_DIM]
        value = turned[:, base + 2 * HEAD_DIM : base + 3 * HEAD_DIM]
        scores = jnp.where(allowed, dot_nt(query, key) * scale, -1e30)
        powers = jnp.exp(scores - jnp.max(scores, axis=1, keepdims=True))
        chances = powers * (1.0 / jnp.sum(powers, axis=1, keepdims=True))
        rounded = chances.astype(jnp.bfloat16)
        attended = dot_nn(rounded, value).astype(jnp.bfloat16)
        out_ref[:, own] = attended
        grad_att = grad_ref[:, own]
        delta = jnp.sum(
            grad_att.astype(jnp.float32) * attended.astype(jnp.float32), axis=1, keepdims=True
        )
        grad_scores = (chances * (dot_nt(grad_att, value) - delta) * scale).astype(jnp.bfloat16)
        grads[:, base : base + HEAD_DIM] = dot_nn(grad_scores, key)
        grads[:, base + HEAD_DIM : base + 2 * HEAD_DIM] = dot_tn(grad_scores, query)
        grads[:, base + 2 * HEAD_DIM : base + 3 * HEAD_DIM] = dot_tn(rounded, grad_att)
    whole = grads[...]
    back_ref[...] = (whole * cos_ref[...] - partner(whole) * sin_ref[...]).astype(jnp.bfloat16)


def attention(qkv, bias, cosines, sines, segment, grad_att, interpret=False):
    packs, size = segment.shape
    columns = qkv.shape[1]
    att_cols = grad_att.shape[1]
    by_rows = lambda width: pl.BlockSpec((size, width), lambda i: (i, 0))
    return pl.pallas_call(
        attention_kernel,
        grid=(packs,),
        in_specs=[
            by_rows(columns),
            pl.BlockSpec((1, columns), lambda i: (0, 0)),
            by_rows(columns),
            by_rows(columns),
            pl.BlockSpec((1, size, 1), lambda i: (i, 0, 0)),
            pl.BlockSpec((1, 1, size), lambda i: (i, 0, 0)),
            by_rows(att_cols),
        ],
        out_specs=[by_rows(att_cols), by_rows(columns)],
        out_shape=[
            jax.ShapeDtypeStruct((packs * size, att_cols), jnp.bfloat16),
            jax.ShapeDtypeStruct((packs * size, columns), jnp.bfloat16),
        ],
        scratch_shapes=[
            pltpu.VMEM((size, columns), jnp.bfloat16),
            pltpu.VMEM((size, columns), jnp.float32),
        ],
        interpret=interpret,
    )(
        qkv,
        bias.reshape(1, columns),
        cosines,
        sines,
        segment.reshape(packs, size, 1),
        segment.reshape(packs, 1, size),
        grad_att,
    )


def add_wide(left, right):
    return (left.astype(jnp.float32) + right.astype(jnp.float32)).astype(left.dtype)


def swap(array, axis, step):
    return lax.ppermute(array, axis, [(i, i ^ step) for i in range(lax.axis_size(axis))])


def total_over(array, axes):
    for axis in axes:
        step = 1
        while step < lax.axis_size(axis):
            array = array + swap(array, axis, step)
            step *= 2
    return array


def line_gather(block, axis):
    count = lax.axis_size(axis)
    here = lax.axis_index(axis)
    ups = [block]
    downs = [block]
    for step in range(count - 1):
        ups.append(lax.ppermute(ups[-1], axis, [(i, i + 1) for i in range(step, count - 1)]))
        downs.append(
            lax.ppermute(downs[-1], axis, [(i + 1, i) for i in range(0, count - 1 - step)])
        )
    zero = (0,) * block.ndim
    stacked = jnp.zeros((count,) + block.shape, block.dtype)
    stacked = lax.dynamic_update_slice(stacked, block[None], (here,) + zero)
    for step in range(1, count):
        piece = jnp.where(here >= step, ups[step], downs[count - step])
        stacked = lax.dynamic_update_slice(stacked, piece[None], ((here - step) % count,) + zero)
    return stacked


def line_scatter(blocks, axis):
    count = lax.axis_size(axis)
    here = lax.axis_index(axis)

    def pick(index):
        return lax.dynamic_index_in_dim(blocks, jnp.clip(index, 0, count - 1), 0, keepdims=False)

    total = pick(here).astype(jnp.float32)
    if count == 1:
        return total
    up = None
    down = None
    for step in range(count - 1):
        send_up = pick(here + count - 1 - step)
        send_down = pick(here - (count - 1) + step)
        if step:
            send_up = add_wide(send_up, up)
            send_down = add_wide(send_down, down)
        up = lax.ppermute(send_up, axis, [(i, i + 1) for i in range(0, step + 1)])
        down = lax.ppermute(
            send_down, axis, [(i + 1, i) for i in range(count - 2 - step, count - 1)]
        )
    return total + up.astype(jnp.float32) + down.astype(jnp.float32)


def grid_gather(block):
    count = lax.axis_size("col")
    if count != 4:
        return [block] + [swap(block, "col", step) for step in range(1, count)]
    cut = block.shape[0] // 2
    by_one = swap(block, "col", 1)
    by_two = swap(block, "col", 2)
    low = swap(by_one[:cut], "col", 2)
    high = swap(by_two[cut:], "col", 1)
    return [block, by_one, by_two, jnp.concatenate([low, high])]


def grid_scatter(part):
    count = lax.axis_size("col")
    size = part.shape[0] // count
    blocks = part.reshape(count, size, part.shape[1])
    if count != 4:
        total = blocks[0]
        for step in range(1, count):
            total = add_wide(total, swap(blocks[step], "col", step))
        return total
    cut = size // 2
    low = swap(jnp.stack([blocks[1, :cut], blocks[3, :cut]]), "col", 1)
    high = swap(jnp.stack([blocks[2, cut:], blocks[3, cut:]]), "col", 2)
    low_last = swap(add_wide(blocks[2, :cut], low[1]), "col", 2)
    high_last = swap(add_wide(blocks[1, cut:], high[1]), "col", 1)
    wide = lambda array: array.astype(jnp.float32)
    return jnp.concatenate(
        [
            (wide(blocks[0, :cut]) + wide(low[0]) + wide(low_last)).astype(part.dtype),
            (wide(blocks[0, cut:]) + wide(high[0]) + wide(high_last)).astype(part.dtype),
        ]
    )


def spread_tokens(block):
    n_col = lax.axis_size("col")
    n_dp = lax.axis_size("dp")
    col = lax.axis_index("col")
    width = block.shape[1]
    groups = line_gather(block, "row").reshape(n_col, -1, width)
    take = lambda step: lax.dynamic_index_in_dim(groups, col ^ step, 0, keepdims=False)
    pieces = [take(0)] + [swap(take(step), "col", step) for step in range(1, n_col)]
    own = jnp.concatenate(pieces, axis=1)
    return jnp.concatenate([own] + [swap(own, "dp", step) for step in range(1, n_dp)])


def collect_tokens(partial):
    n_col = lax.axis_size("col")
    n_dp = lax.axis_size("dp")
    n_row = lax.axis_size("row")
    col = lax.axis_index("col")
    tokens = partial.shape[0] // n_dp
    width = partial.shape[1] // n_col
    summed = partial[:tokens]
    for step in range(1, n_dp):
        summed = add_wide(summed, swap(partial[step * tokens : (step + 1) * tokens], "dp", step))
    groups = jnp.zeros((n_col, tokens, width), partial.dtype)
    for step in range(n_col):
        piece = summed[:, step * width : (step + 1) * width]
        if step:
            piece = swap(piece, "col", step)
        groups = lax.dynamic_update_slice(groups, piece[None], (col ^ step, 0, 0))
    return line_scatter(groups.reshape(n_row, -1, width), "row")


def half_of(array, axis):
    size = array.shape[axis] // lax.axis_size("dp")
    return lax.dynamic_slice_in_dim(array, lax.axis_index("dp") * size, size, axis)


def both_halves(own, axis):
    n_dp = lax.axis_size("dp")
    here = lax.axis_index("dp")
    parts = [own] + [swap(own, "dp", step) for step in range(1, n_dp)]
    if n_dp == 2:
        low = jnp.where(here == 0, parts[0], parts[1])
        high = jnp.where(here == 0, parts[1], parts[0])
        return jnp.concatenate([low, high], axis=axis)
    size = own.shape[axis]
    out = jnp.concatenate(parts, axis=axis)
    for step in range(n_dp):
        out = lax.dynamic_update_slice_in_dim(out, parts[step], (here ^ step) * size, axis)
    return out


def body(
    inputs,
    segment,
    grad_output,
    norm_gain,
    norm_bias,
    qkv_weight,
    qkv_bias,
    dense_weight,
    dense_bias,
    fc1_weight,
    fc1_bias,
    fc2_weight,
    fc2_bias,
):
    n_col = lax.axis_size("col")
    n_dp = lax.axis_size("dp")
    width = inputs.shape[1]
    full_width = n_col * width
    qkv_cols = qkv_weight.shape[1] // n_dp
    att_cols = dense_weight.shape[0] // n_dp
    grad_rows = spread_tokens(grad_output)
    in_half = jnp.concatenate([half_of(qkv_weight, 1), half_of(fc1_weight, 1)], axis=1)
    back_half = jnp.concatenate([half_of(dense_weight, 0), half_of(fc2_weight, 0)], axis=0)
    in_all = jnp.concatenate(grid_gather(in_half))
    back_all = jnp.concatenate(grid_gather(back_half), axis=1)

    wide_in = inputs.astype(jnp.float32)
    sums = total_over(
        jnp.stack([jnp.sum(wide_in, axis=1), jnp.sum(wide_in * wide_in, axis=1)]), ("col",)
    )
    row_mean = (sums[0] / full_width)[:, None]
    row_square = (sums[1] / full_width)[:, None]
    inv_std = lax.rsqrt(row_square - row_mean * row_mean + EPS)
    centered = (wide_in - row_mean) * inv_std
    normed = (centered * norm_gain + norm_bias).astype(jnp.bfloat16)
    normed_rows = spread_tokens(normed)
    seg_rows = jnp.concatenate([segment] + [swap(segment, "dp", step) for step in range(1, n_dp)])
    cosines, sines = rotary_tables(seg_rows, qkv_cols)

    projected = dot_nn(normed_rows, in_all)
    pre_act = projected[:, qkv_cols:] + half_of(fc1_bias, 0)
    hidden = gelu_tanh(pre_act).astype(jnp.bfloat16)
    backed = dot_nt(grad_rows, back_all)
    grad_att = backed[:, :att_cols].astype(jnp.bfloat16)
    grad_fc2_t = grid_scatter(dot_tn(grad_rows, hidden).astype(jnp.bfloat16))
    grad_pre = (backed[:, att_cols:] * gelu_slope(pre_act)).astype(jnp.bfloat16)
    grad_fc1 = grid_scatter(dot_tn(normed_rows, grad_pre).astype(jnp.bfloat16))

    attended, grad_qkv = attention(
        projected[:, :qkv_cols], half_of(qkv_bias, 0), cosines, sines, seg_rows, grad_att
    )
    acts = jnp.concatenate([attended, hidden], axis=1)
    mixed = collect_tokens(dot_nn(acts, back_all).astype(jnp.bfloat16))
    output = (wide_in + (mixed + dense_bias + fc2_bias)).astype(jnp.bfloat16)

    grad_first = jnp.concatenate([grad_qkv, grad_pre], axis=1)
    grad_normed = collect_tokens(dot_nt(grad_first, in_all).astype(jnp.bfloat16))
    late = grid_scatter(
        jnp.concatenate(
            [
                dot_tn(normed_rows, grad_qkv).astype(jnp.bfloat16),
                dot_tn(grad_rows, attended).astype(jnp.bfloat16),
            ],
            axis=1,
        )
    )
    grad_in_b = total_over(jnp.sum(grad_first.astype(jnp.float32), axis=0, keepdims=True), ("col",))

    scaled = grad_normed * norm_gain
    cross = total_over(
        jnp.stack([jnp.sum(scaled, axis=1), jnp.sum(scaled * centered, axis=1)]), ("col",)
    )
    grad_wide = grad_output.astype(jnp.float32)
    grad_input = grad_wide + inv_std * (
        scaled - (cross[0] / full_width)[:, None] - centered * (cross[1] / full_width)[:, None]
    )
    norm_sums = total_over(
        jnp.stack(
            [
                jnp.sum(grad_normed * centered, axis=0),
                jnp.sum(grad_normed, axis=0),
                jnp.sum(grad_wide, axis=0),
            ]
        ),
        ("dp", "row"),
    )
    wide = lambda array: array.astype(jnp.float32)
    return (
        output,
        grad_input,
        norm_sums[0],
        norm_sums[1],
        wide(both_halves(late[:, :qkv_cols], 1)),
        both_halves(grad_in_b[0, :qkv_cols], 0),
        wide(both_halves(late[:, qkv_cols:].T, 0)),
        norm_sums[2],
        wide(both_halves(grad_fc1, 1)),
        both_halves(grad_in_b[0, qkv_cols:], 0),
        wide(both_halves(grad_fc2_t.T, 0)),
        norm_sums[2],
    )


def solution(mesh):
    in_specs = (
        P(("dp", "row"), "col"),
        P(("dp", "col"), None),
        P(("dp", "row"), "col"),
        P("col"),
        P("col"),
        P("col", "row"),
        P("row"),
        P("row", "col"),
        P("col"),
        P("col", "row"),
        P("row"),
        P("row", "col"),
        P("col"),
    )
    out_specs = (
        P(("dp", "row"), "col"),
        P(("dp", "row"), "col"),
        P("col"),
        P("col"),
        P("col", "row"),
        P("row"),
        P("row", "col"),
        P("col"),
        P("col", "row"),
        P("row"),
        P("row", "col"),
        P("col"),
    )
    return jax.shard_map(body, mesh=mesh, in_specs=in_specs, out_specs=out_specs, check_vma=False)
```

```python
import math

import jax
import jax.numpy as jnp
from jax import lax
from jax.experimental import pallas as pl
from jax.experimental.pallas import tpu as pltpu
from jax.sharding import PartitionSpec as P


HEAD_DIM = 64
ROT = 32


EPS = 1e-05


def gelu_tanh(values):
    inner = 0.7978845608028654 * (values + 0.044715 * values * values * values)
    return 0.5 * values * (1.0 + jnp.tanh(inner))


def gelu_slope(values):
    inner = 0.7978845608028654 * (values + 0.044715 * values * values * values)
    tangent = jnp.tanh(inner)
    return 0.5 * (1.0 + tangent) + 0.5 * values * (1.0 - tangent * tangent) * 0.7978845608028654 * (
        1.0 + 0.134145 * values * values
    )


def rotary_tables(segment, columns):
    width = segment.shape[1]
    places = jnp.arange(width, dtype=jnp.int32)
    fresh = jnp.concatenate(
        [jnp.ones((segment.shape[0], 1), dtype=jnp.bool_), segment[:, 1:] != segment[:, :-1]],
        axis=1,
    )
    starts = lax.cummax(jnp.where(fresh, places[None, :], jnp.zeros_like(segment)), axis=1)
    offsets = (places[None, :] - starts).astype(jnp.float32).reshape(-1, 1)
    half_rot = ROT // 2
    column = jnp.arange(3 * HEAD_DIM, dtype=jnp.int32)
    part = column % HEAD_DIM
    turned = (column < 2 * HEAD_DIM) & (part < ROT)
    freqs = jnp.exp((part % half_rot).astype(jnp.float32) * (-2.0 * math.log(10000.0) / ROT))
    freqs = jnp.where(turned, freqs, 0.0)
    sign = jnp.where(turned, jnp.where(part < half_rot, -1.0, 1.0), 0.0)
    angles = offsets * freqs[None, :]
    repeats = columns // (3 * HEAD_DIM)
    cosines = jnp.concatenate([jnp.cos(angles)] * repeats, axis=1)
    sines = jnp.concatenate([jnp.sin(angles) * sign[None, :]] * repeats, axis=1)
    return cosines, sines


def dot_nt(left, right):
    return lax.dot_general(
        left, right, (((1,), (1,)), ((), ())), preferred_element_type=jnp.float32
    )


def dot_tn(left, right):
    return lax.dot_general(
        left, right, (((0,), (0,)), ((), ())), preferred_element_type=jnp.float32
    )


def dot_nn(left, right):
    return jnp.dot(left, right, preferred_element_type=jnp.float32)


def attention_kernel(
    qkv_ref, bias_ref, cos_ref, sin_ref, seg_col_ref, seg_row_ref, grad_ref, out_ref, back_ref, turned, grads
):
    heads = out_ref.shape[1] // HEAD_DIM
    columns = qkv_ref.shape[1]
    half_rot = ROT // 2
    lanes = lax.broadcasted_iota(jnp.int32, (1, columns), 1) % HEAD_DIM
    first = lanes < half_rot

    def partner(values):
        ahead = pltpu.roll(values, columns - half_rot, 1)
        behind = pltpu.roll(values, half_rot, 1)
        return jnp.where(first, ahead, behind)

    full = qkv_ref[...] + bias_ref[...]
    turned[...] = (full * cos_ref[...] + partner(full) * sin_ref[...]).astype(jnp.bfloat16)
    size = qkv_ref.shape[0]
    rows = lax.broadcasted_iota(jnp.int32, (size, size), 0)
    places = lax.broadcasted_iota(jnp.int32, (size, size), 1)
    allowed = (seg_col_ref[0] == seg_row_ref[0]) & (places <= rows)
    scale = HEAD_DIM ** (-0.5)
    for head in range(heads):
        base = head * 3 * HEAD_DIM
        own = slice(head * HEAD_DIM, (head + 1) * HEAD_DIM)
        query = turned[:, base : base + HEAD_DIM]
        key = turned[:, base + HEAD_DIM : base + 2 * HEAD_DIM]
        value = turned[:, base + 2 * HEAD_DIM : base + 3 * HEAD_DIM]
        scores = jnp.where(allowed, dot_nt(query, key) * scale, -1e30)
        powers = jnp.exp(scores - jnp.max(scores, axis=1, keepdims=True))
        chances = powers * (1.0 / jnp.sum(powers, axis=1, keepdims=True))
        rounded = chances.astype(jnp.bfloat16)
        attended = dot_nn(rounded, value).astype(jnp.bfloat16)
        out_ref[:, own] = attended
        grad_att = grad_ref[:, own]
        delta = jnp.sum(
            grad_att.astype(jnp.float32) * attended.astype(jnp.float32), axis=1, keepdims=True
        )
        grad_scores = (chances * (dot_nt(grad_att, value) - delta) * scale).astype(jnp.bfloat16)
        grads[:, base : base + HEAD_DIM] = dot_nn(grad_scores, key)
        grads[:, base + HEAD_DIM : base + 2 * HEAD_DIM] = dot_tn(grad_scores, query)
        grads[:, base + 2 * HEAD_DIM : base + 3 * HEAD_DIM] = dot_tn(rounded, grad_att)
    whole = grads[...]
    back_ref[...] = (whole * cos_ref[...] - partner(whole) * sin_ref[...]).astype(jnp.bfloat16)


def attention(qkv, bias, cosines, sines, segment, grad_att, interpret=False):
    packs, size = segment.shape
    columns = qkv.shape[1]
    att_cols = grad_att.shape[1]
    by_rows = lambda width: pl.BlockSpec((size, width), lambda i: (i, 0))
    return pl.pallas_call(
        attention_kernel,
        grid=(packs,),
        in_specs=[
            by_rows(columns),
            pl.BlockSpec((1, columns), lambda i: (0, 0)),
            by_rows(columns),
            by_rows(columns),
            pl.BlockSpec((1, size, 1), lambda i: (i, 0, 0)),
            pl.BlockSpec((1, 1, size), lambda i: (i, 0, 0)),
            by_rows(att_cols),
        ],
        out_specs=[by_rows(att_cols), by_rows(columns)],
        out_shape=[
            jax.ShapeDtypeStruct((packs * size, att_cols), jnp.bfloat16),
            jax.ShapeDtypeStruct((packs * size, columns), jnp.bfloat16),
        ],
        scratch_shapes=[
            pltpu.VMEM((size, columns), jnp.bfloat16),
            pltpu.VMEM((size, columns), jnp.float32),
        ],
        interpret=interpret,
    )(
        qkv,
        bias.reshape(1, columns),
        cosines,
        sines,
        segment.reshape(packs, size, 1),
        segment.reshape(packs, 1, size),
        grad_att,
    )


def add_wide(left, right):
    return (left.astype(jnp.float32) + right.astype(jnp.float32)).astype(left.dtype)


def swap(array, axis, step):
    return lax.ppermute(array, axis, [(i, i ^ step) for i in range(lax.axis_size(axis))])


def total_over(array, axes, *late):
    number = 0
    for axis in axes:
        step = 1
        while step < lax.axis_size(axis):
            number += 1
            other = swap(array, axis, step)
            if number <= len(late):
                other = lax.optimization_barrier((other, late[number - 1]))[0]
            array = array + other
            step *= 2
    return array


def after(value, *others):
    return lax.optimization_barrier((value,) + others)[0]


def grid_gather(block):
    count = lax.axis_size("col")
    if count != 4:
        got = [swap(block, "col", step) for step in range(1, count)]
        return [block] + got, got
    cut = block.shape[0] // 2
    by_one = swap(block, "col", 1)
    by_two = swap(block, "col", 2)
    low = swap(by_one[:cut], "col", 2)
    high = swap(by_two[cut:], "col", 1)
    return [block, by_one, by_two, jnp.concatenate([low, high])], [by_one, by_two]


def scatter_first(part):
    count = lax.axis_size("col")
    size = part.shape[0] // count
    blocks = part.reshape(count, size, part.shape[1])
    if count != 4:
        return [blocks[0]], [swap(blocks[step], "col", step) for step in range(1, count)]
    cut = size // 2
    low = swap(jnp.stack([blocks[1, :cut], blocks[3, :cut]]), "col", 1)
    high = swap(jnp.stack([blocks[2, cut:], blocks[3, cut:]]), "col", 2)
    return [blocks[0, :cut], blocks[0, cut:], blocks[2, :cut], blocks[1, cut:]], [low, high]


def scatter_second(kept, got):
    if lax.axis_size("col") != 4:
        return [], kept + got
    low, high = got
    low_sum = add_wide(kept[2], low[1])
    high_sum = add_wide(kept[3], high[1])
    low_last = swap(low_sum, "col", 2)
    high_last = swap(high_sum, "col", 1)
    return [low_sum, high_sum], [kept[0], low[0], low_last, kept[1], high[0], high_last]


def scatter_last(parts):
    def total(arrays):
        out = arrays[0].astype(jnp.float32)
        for array in arrays[1:]:
            out = out + array.astype(jnp.float32)
        return out.astype(arrays[0].dtype)

    if lax.axis_size("col") != 4:
        return total(parts)
    return jnp.concatenate([total(parts[:3]), total(parts[3:])])


def place(row, col, n_col):
    return row * n_col + col


def spread_start(block):
    n_col = lax.axis_size("col")
    n_row = lax.axis_size("row")
    deep = n_row // n_col
    pieces = []
    for low in range(deep):
        for step in range(n_col):
            pairs = []
            for to_row in range(n_row):
                for to_col in range(n_col):
                    from_row = to_col * deep + ((to_row % deep) ^ low)
                    from_col = (to_row // deep) ^ step
                    pairs.append(
                        (place(from_row, from_col, n_col), place(to_row, to_col, n_col))
                    )
            pieces.append(lax.ppermute(block, ("row", "col"), pairs))
    return pieces


def spread_finish(pieces):
    n_col = lax.axis_size("col")
    deep = lax.axis_size("row") // n_col
    row = lax.axis_index("row")
    tokens, width = pieces[0].shape
    wide = jnp.zeros((deep * tokens, n_col * width), pieces[0].dtype)
    offset = (row // deep) ^ lax.axis_index("col")
    for number, piece in enumerate(pieces):
        at_row = ((row % deep) ^ (number // n_col)) * tokens
        at_col = (offset ^ (number % n_col)) * width
        wide = lax.dynamic_update_slice(wide, piece, (at_row, at_col))
    return wide


def dp_parts(own):
    return [own] + [swap(own, "dp", step) for step in range(1, lax.axis_size("dp"))]


def collect_first(partial):
    n_dp = lax.axis_size("dp")
    tokens = partial.shape[0] // n_dp
    summed = partial[:tokens]
    for step in range(1, n_dp):
        other = swap(partial[step * tokens : (step + 1) * tokens], "dp", step)
        summed = add_wide(summed, other)
    return summed


def collect_second(summed):
    n_col = lax.axis_size("col")
    col = lax.axis_index("col")
    tokens = summed.shape[0]
    width = summed.shape[1] // n_col
    groups = jnp.zeros((n_col, tokens, width), summed.dtype)
    for step in range(n_col):
        piece = summed[:, step * width : (step + 1) * width]
        if step:
            piece = swap(piece, "col", step)
        groups = lax.dynamic_update_slice(groups, piece[None], (col ^ step, 0, 0))
    return groups


def collect_third(groups):
    n_row = lax.axis_size("row")
    row = lax.axis_index("row")
    blocks = groups.reshape(n_row, -1, groups.shape[-1])
    take = lambda step: lax.dynamic_index_in_dim(blocks, row ^ step, 0, keepdims=False)
    held = {step: take(step) for step in range(n_row)}
    bit = 1
    while bit < n_row:
        sent = jnp.stack([held[step] for step in sorted(held) if step & bit])
        got = swap(sent, "row", bit)
        kept = [step for step in sorted(held) if not step & bit]
        last = 2 * bit >= n_row
        held = {
            step: held[step].astype(jnp.float32) + got[place].astype(jnp.float32)
            for place, step in enumerate(kept)
        }
        if not last:
            held = {step: value.astype(groups.dtype) for step, value in held.items()}
        bit *= 2
    return held[0].astype(jnp.float32)


def late_kernel(*refs):
    out_ref = refs[-1]
    count = len(refs) // 4
    split = refs[count].shape[1]

    def total(lefts, rights):
        out = dot_tn(lefts[0][...], rights[0][...])
        for left, right in zip(lefts[1:], rights[1:]):
            out = out + dot_tn(left[...], right[...])
        return out.astype(jnp.bfloat16)

    out_ref[:, :split] = total(refs[:count], refs[count : 2 * count])
    out_ref[:, split:] = total(refs[2 * count : 3 * count], refs[3 * count : 4 * count])


def late_grads(normed_parts, grad_qkv, grad_parts, attended):
    tokens, full = normed_parts[0].shape
    count = len(normed_parts)
    columns = grad_qkv.shape[1] + attended.shape[1]
    tile = 512
    left = [pl.BlockSpec((tokens, tile), lambda i: (0, i))] * count
    right = lambda array: [
        pl.BlockSpec((tokens, array.shape[1]), lambda i, part=part: (part, 0))
        for part in range(count)
    ]
    return pl.pallas_call(
        late_kernel,
        grid=(full // tile,),
        in_specs=left + right(grad_qkv) + left + right(attended),
        out_specs=pl.BlockSpec((tile, columns), lambda i: (i, 0)),
        out_shape=jax.ShapeDtypeStruct((full, columns), jnp.bfloat16),
    )(*normed_parts, *[grad_qkv] * count, *grad_parts, *[attended] * count)


def half_of(array, axis):
    size = array.shape[axis] // lax.axis_size("dp")
    return lax.dynamic_slice_in_dim(array, lax.axis_index("dp") * size, size, axis)


def both_halves(own, axis):
    n_dp = lax.axis_size("dp")
    here = lax.axis_index("dp")
    parts = [own] + [swap(own, "dp", step) for step in range(1, n_dp)]
    if n_dp == 2:
        low = jnp.where(here == 0, parts[0], parts[1])
        high = jnp.where(here == 0, parts[1], parts[0])
        return jnp.concatenate([low, high], axis=axis)
    size = own.shape[axis]
    out = jnp.concatenate(parts, axis=axis)
    for step in range(n_dp):
        out = lax.dynamic_update_slice_in_dim(out, parts[step], (here ^ step) * size, axis)
    return out


def body(
    inputs,
    segment,
    grad_output,
    norm_gain,
    norm_bias,
    qkv_weight,
    qkv_bias,
    dense_weight,
    dense_bias,
    fc1_weight,
    fc1_bias,
    fc2_weight,
    fc2_bias,
):
    n_col = lax.axis_size("col")
    n_dp = lax.axis_size("dp")
    width = inputs.shape[1]
    full_width = n_col * width
    qkv_cols = qkv_weight.shape[1] // n_dp
    att_cols = dense_weight.shape[0] // n_dp
    wide_in = inputs.astype(jnp.float32)
    own_sums = jnp.stack([jnp.sum(wide_in, axis=1), jnp.sum(wide_in * wide_in, axis=1)])
    scales = jnp.stack([norm_gain, norm_bias])
    scales = jnp.concatenate(
        [scales]
        + [swap(scales, "col", step) for step in range(1, n_col)],
        axis=1,
    )
    in_pieces = spread_start(inputs)
    fc1_blocks, fc1_early = grid_gather(half_of(fc1_weight, 1))
    grad_pieces = spread_start(grad_output)
    back_half = jnp.concatenate([half_of(dense_weight, 0), half_of(fc2_weight, 0)], axis=0)
    back_blocks, back_early = grid_gather(after(back_half, *fc1_early))
    qkv_blocks, _ = grid_gather(after(half_of(qkv_weight, 1), *back_early))
    fc1_all = jnp.concatenate(fc1_blocks)
    back_all = jnp.concatenate(back_blocks, axis=1)
    qkv_all = jnp.concatenate(qkv_blocks)
    seg_rows = jnp.concatenate(dp_parts(segment))
    cosines, sines = rotary_tables(seg_rows, qkv_cols)

    def centre(wide_in, row_total, row_squares):
        row_mean = (row_total / full_width)[:, None]
        row_square = (row_squares / full_width)[:, None]
        inv_std = lax.rsqrt(row_square - row_mean * row_mean + EPS)
        return (wide_in - row_mean) * inv_std, inv_std

    in_pieces = list(
        lax.optimization_barrier(tuple(in_pieces) + (cosines, sines))[:-2]
    )
    wide_rows = spread_finish(in_pieces).astype(jnp.float32)
    centered_rows, _ = centre(
        wide_rows, jnp.sum(wide_rows, axis=1), jnp.sum(wide_rows * wide_rows, axis=1)
    )
    normed_own = (centered_rows * scales[:1] + scales[1:]).astype(jnp.bfloat16)
    normed_parts = dp_parts(normed_own)
    normed_rows = jnp.concatenate(normed_parts)

    fc1_shift = half_of(fc1_bias, 0)
    pre_act = dot_nn(normed_rows, fc1_all) + fc1_shift
    hidden = gelu_tanh(pre_act).astype(jnp.bfloat16)
    grad_pieces = list(lax.optimization_barrier(tuple(grad_pieces) + (normed_own,))[:-1])
    grad_parts = dp_parts(spread_finish(grad_pieces))
    grad_rows = jnp.concatenate(grad_parts)
    fc2_part = dot_tn(grad_rows, hidden).astype(jnp.bfloat16)
    fc2_kept, fc2_got = scatter_first(fc2_part)

    backed = dot_nt(after(grad_rows, fc2_part), back_all)
    grad_att = backed[:, :att_cols].astype(jnp.bfloat16)
    grad_pre = (backed[:, att_cols:] * gelu_slope(pre_act)).astype(jnp.bfloat16)
    fc1_part = dot_tn(normed_rows, grad_pre).astype(jnp.bfloat16)
    fc1_kept, fc1_got = scatter_first(fc1_part)

    attended, grad_qkv = attention(
        after(dot_nn(normed_rows, qkv_all), fc1_part),
        half_of(qkv_bias, 0),
        cosines,
        sines,
        seg_rows,
        grad_att,
    )
    bias_sums = jnp.concatenate(
        [
            jnp.sum(grad_qkv.astype(jnp.float32), axis=0, keepdims=True),
            jnp.sum(grad_pre.astype(jnp.float32), axis=0, keepdims=True),
        ],
        axis=1,
    )
    fc2_got = list(lax.optimization_barrier((tuple(fc2_got), grad_qkv))[0])
    fc2_sent, fc2_parts = scatter_second(fc2_kept, fc2_got)
    fc1_got = list(lax.optimization_barrier((tuple(fc1_got), grad_qkv))[0])
    fc1_sent, fc1_parts = scatter_second(fc1_kept, fc1_got)
    norm_part = (
        dot_nt(after(grad_qkv, *fc2_sent), qkv_all) + dot_nt(after(grad_pre, fc1_part), fc1_all)
    ).astype(jnp.bfloat16)
    norm_summed = collect_first(norm_part)
    acts = after(jnp.concatenate([attended, hidden], axis=1), norm_summed, *fc1_sent)
    mixed_part = dot_nn(acts, back_all).astype(jnp.bfloat16)
    mixed_summed = after(collect_first(mixed_part), norm_summed)
    norm_groups = collect_second(norm_summed)
    mixed_groups = collect_second(mixed_summed)

    late_part = late_grads(
        normed_parts, after(grad_qkv, mixed_summed), grad_parts, attended
    )
    late_kept, late_got = scatter_first(late_part)
    norm_groups = after(norm_groups, late_part)
    grad_normed = collect_third(norm_groups)
    mixed_groups = after(mixed_groups, norm_groups)
    mixed = collect_third(mixed_groups)
    late_got = list(lax.optimization_barrier((tuple(late_got), mixed_groups))[0])
    late_sent, late_parts = scatter_second(late_kept, late_got)

    fc2_parts = lax.optimization_barrier((tuple(fc2_parts), tuple(late_sent)))[0]
    grad_fc2_t = scatter_last(list(fc2_parts))
    fc1_parts = lax.optimization_barrier((tuple(fc1_parts), grad_fc2_t))[0]
    grad_fc1 = scatter_last(list(fc1_parts))
    wide = lambda array: array.astype(jnp.float32)
    out_fc1 = wide(both_halves(grad_fc1, 1))
    out_fc2 = wide(both_halves(grad_fc2_t.T, 0))
    grad_normed = after(grad_normed, out_fc1, out_fc2, *late_sent)
    late = scatter_last(list(lax.optimization_barrier((tuple(late_parts), grad_normed))[0]))

    grad_in_b = total_over(bias_sums, ("col",), norm_groups, grad_fc1)
    sums = total_over(own_sums, ("col",), scales, late_part)
    centered, inv_std = centre(wide_in, sums[0], sums[1])
    scaled = grad_normed * norm_gain
    cross = total_over(
        jnp.stack([jnp.sum(scaled, axis=1), jnp.sum(scaled * centered, axis=1)]), ("col",)
    )
    grad_wide = grad_output.astype(jnp.float32)
    grad_input = grad_wide + inv_std * (
        scaled - (cross[0] / full_width)[:, None] - centered * (cross[1] / full_width)[:, None]
    )
    own_norm = jnp.stack(
        [
            jnp.sum(grad_normed * centered, axis=0),
            jnp.sum(grad_normed, axis=0),
            jnp.sum(grad_wide, axis=0),
        ]
    )
    norm_sums = total_over(own_norm, ("dp", "row"))
    mixed = after(mixed, own_norm)
    output = (wide_in + (mixed + dense_bias + fc2_bias)).astype(jnp.bfloat16)
    return (
        output,
        grad_input,
        norm_sums[0],
        norm_sums[1],
        wide(both_halves(late[:, :qkv_cols], 1)),
        both_halves(grad_in_b[0, :qkv_cols], 0),
        wide(both_halves(late[:, qkv_cols:].T, 0)),
        norm_sums[2],
        out_fc1,
        both_halves(grad_in_b[0, qkv_cols:], 0),
        out_fc2,
        norm_sums[2],
    )


def solution(mesh):
    in_specs = (
        P(("dp", "row"), "col"),
        P(("dp", "col"), None),
        P(("dp", "row"), "col"),
        P("col"),
        P("col"),
        P("col", "row"),
        P("row"),
        P("row", "col"),
        P("col"),
        P("col", "row"),
        P("row"),
        P("row", "col"),
        P("col"),
    )
    out_specs = (
        P(("dp", "row"), "col"),
        P(("dp", "row"), "col"),
        P("col"),
        P("col"),
        P("col", "row"),
        P("row"),
        P("row", "col"),
        P("col"),
        P("col", "row"),
        P("row"),
        P("row", "col"),
        P("col"),
    )

    return jax.shard_map(body, mesh=mesh, in_specs=in_specs, out_specs=out_specs, check_vma=False)
```

```python
import math

import jax
import jax.numpy as jnp
from jax import lax
from jax.experimental import pallas as pl
from jax.experimental.pallas import tpu as pltpu
from jax.sharding import PartitionSpec as P


HEAD_DIM = 64
ROT = 32


EPS = 1e-05


def gelu_tanh(values):
    inner = 0.7978845608028654 * (values + 0.044715 * values * values * values)
    return 0.5 * values * (1.0 + jnp.tanh(inner))


def gelu_slope(values):
    inner = 0.7978845608028654 * (values + 0.044715 * values * values * values)
    tangent = jnp.tanh(inner)
    return 0.5 * (1.0 + tangent) + 0.5 * values * (1.0 - tangent * tangent) * 0.7978845608028654 * (
        1.0 + 0.134145 * values * values
    )


def rotary_tables(segment, columns):
    width = segment.shape[1]
    places = jnp.arange(width, dtype=jnp.int32)
    fresh = jnp.concatenate(
        [jnp.ones((segment.shape[0], 1), dtype=jnp.bool_), segment[:, 1:] != segment[:, :-1]],
        axis=1,
    )
    starts = lax.cummax(jnp.where(fresh, places[None, :], jnp.zeros_like(segment)), axis=1)
    offsets = (places[None, :] - starts).astype(jnp.float32).reshape(-1, 1)
    half_rot = ROT // 2
    column = jnp.arange(3 * HEAD_DIM, dtype=jnp.int32)
    part = column % HEAD_DIM
    turned = (column < 2 * HEAD_DIM) & (part < ROT)
    freqs = jnp.exp((part % half_rot).astype(jnp.float32) * (-2.0 * math.log(10000.0) / ROT))
    freqs = jnp.where(turned, freqs, 0.0)
    sign = jnp.where(turned, jnp.where(part < half_rot, -1.0, 1.0), 0.0)
    angles = offsets * freqs[None, :]
    repeats = columns // (3 * HEAD_DIM)
    cosines = jnp.concatenate([jnp.cos(angles)] * repeats, axis=1)
    sines = jnp.concatenate([jnp.sin(angles) * sign[None, :]] * repeats, axis=1)
    return cosines, sines


def dot_nt(left, right):
    return lax.dot_general(
        left, right, (((1,), (1,)), ((), ())), preferred_element_type=jnp.float32
    )


def dot_tn(left, right):
    return lax.dot_general(
        left, right, (((0,), (0,)), ((), ())), preferred_element_type=jnp.float32
    )


def dot_nn(left, right):
    return jnp.dot(left, right, preferred_element_type=jnp.float32)


def attention_kernel(
    qkv_ref, bias_ref, cos_ref, sin_ref, seg_col_ref, seg_row_ref, grad_ref, out_ref, back_ref, turned, grads
):
    heads = out_ref.shape[1] // HEAD_DIM
    columns = qkv_ref.shape[1]
    half_rot = ROT // 2
    lanes = lax.broadcasted_iota(jnp.int32, (1, columns), 1) % HEAD_DIM
    first = lanes < half_rot

    def partner(values):
        ahead = pltpu.roll(values, columns - half_rot, 1)
        behind = pltpu.roll(values, half_rot, 1)
        return jnp.where(first, ahead, behind)

    full = qkv_ref[...] + bias_ref[...]
    turned[...] = (full * cos_ref[...] + partner(full) * sin_ref[...]).astype(jnp.bfloat16)
    size = qkv_ref.shape[0]
    rows = lax.broadcasted_iota(jnp.int32, (size, size), 0)
    places = lax.broadcasted_iota(jnp.int32, (size, size), 1)
    allowed = (seg_col_ref[0] == seg_row_ref[0]) & (places <= rows)
    scale = HEAD_DIM ** (-0.5)
    for head in range(heads):
        base = head * 3 * HEAD_DIM
        own = slice(head * HEAD_DIM, (head + 1) * HEAD_DIM)
        query = turned[:, base : base + HEAD_DIM]
        key = turned[:, base + HEAD_DIM : base + 2 * HEAD_DIM]
        value = turned[:, base + 2 * HEAD_DIM : base + 3 * HEAD_DIM]
        scores = jnp.where(allowed, dot_nt(query, key) * scale, -1e30)
        powers = jnp.exp(scores - jnp.max(scores, axis=1, keepdims=True))
        chances = powers * (1.0 / jnp.sum(powers, axis=1, keepdims=True))
        rounded = chances.astype(jnp.bfloat16)
        attended = dot_nn(rounded, value).astype(jnp.bfloat16)
        out_ref[:, own] = attended
        grad_att = grad_ref[:, own]
        delta = jnp.sum(
            grad_att.astype(jnp.float32) * attended.astype(jnp.float32), axis=1, keepdims=True
        )
        grad_scores = (chances * (dot_nt(grad_att, value) - delta) * scale).astype(jnp.bfloat16)
        grads[:, base : base + HEAD_DIM] = dot_nn(grad_scores, key)
        grads[:, base + HEAD_DIM : base + 2 * HEAD_DIM] = dot_tn(grad_scores, query)
        grads[:, base + 2 * HEAD_DIM : base + 3 * HEAD_DIM] = dot_tn(rounded, grad_att)
    whole = grads[...]
    back_ref[...] = (whole * cos_ref[...] - partner(whole) * sin_ref[...]).astype(jnp.bfloat16)


def attention(qkv, bias, cosines, sines, segment, grad_att, interpret=False):
    packs, size = segment.shape
    columns = qkv.shape[1]
    att_cols = grad_att.shape[1]
    by_rows = lambda width: pl.BlockSpec((size, width), lambda i: (i, 0))
    return pl.pallas_call(
        attention_kernel,
        grid=(packs,),
        in_specs=[
            by_rows(columns),
            pl.BlockSpec((1, columns), lambda i: (0, 0)),
            by_rows(columns),
            by_rows(columns),
            pl.BlockSpec((1, size, 1), lambda i: (i, 0, 0)),
            pl.BlockSpec((1, 1, size), lambda i: (i, 0, 0)),
            by_rows(att_cols),
        ],
        out_specs=[by_rows(att_cols), by_rows(columns)],
        out_shape=[
            jax.ShapeDtypeStruct((packs * size, att_cols), jnp.bfloat16),
            jax.ShapeDtypeStruct((packs * size, columns), jnp.bfloat16),
        ],
        scratch_shapes=[
            pltpu.VMEM((size, columns), jnp.bfloat16),
            pltpu.VMEM((size, columns), jnp.float32),
        ],
        interpret=interpret,
    )(
        qkv,
        bias.reshape(1, columns),
        cosines,
        sines,
        segment.reshape(packs, size, 1),
        segment.reshape(packs, 1, size),
        grad_att,
    )


def add_wide(left, right):
    return (left.astype(jnp.float32) + right.astype(jnp.float32)).astype(left.dtype)


def swap(array, axis, step):
    return lax.ppermute(array, axis, [(i, i ^ step) for i in range(lax.axis_size(axis))])


def total_over(array, axes, *late):
    number = 0
    for axis in axes:
        step = 1
        while step < lax.axis_size(axis):
            number += 1
            other = swap(array, axis, step)
            if number <= len(late):
                other = lax.optimization_barrier((other, late[number - 1]))[0]
            array = array + other
            step *= 2
    return array


def after(value, *others):
    return lax.optimization_barrier((value,) + others)[0]


def grid_gather(block):
    count = lax.axis_size("col")
    if count != 4:
        got = [swap(block, "col", step) for step in range(1, count)]
        return [block] + got, got
    cut = block.shape[0] // 2
    by_one = swap(block, "col", 1)
    by_two = swap(block, "col", 2)
    low = swap(by_one[:cut], "col", 2)
    high = swap(by_two[cut:], "col", 1)
    return [block, by_one, by_two, jnp.concatenate([low, high])], [by_one, by_two]


def scatter_first(part):
    count = lax.axis_size("col")
    size = part.shape[0] // count
    blocks = part.reshape(count, size, part.shape[1])
    if count != 4:
        return [blocks[0]], [swap(blocks[step], "col", step) for step in range(1, count)]
    cut = size // 2
    low = swap(jnp.stack([blocks[1, :cut], blocks[3, :cut]]), "col", 1)
    high = swap(jnp.stack([blocks[2, cut:], blocks[3, cut:]]), "col", 2)
    return [blocks[0, :cut], blocks[0, cut:], blocks[2, :cut], blocks[1, cut:]], [low, high]


def scatter_second(kept, got):
    if lax.axis_size("col") != 4:
        return [], kept + got
    low, high = got
    low_sum = add_wide(kept[2], low[1])
    high_sum = add_wide(kept[3], high[1])
    low_last = swap(low_sum, "col", 2)
    high_last = swap(high_sum, "col", 1)
    return [low_sum, high_sum], [kept[0], low[0], low_last, kept[1], high[0], high_last]


def scatter_last(parts):
    def total(arrays):
        out = arrays[0].astype(jnp.float32)
        for array in arrays[1:]:
            out = out + array.astype(jnp.float32)
        return out.astype(arrays[0].dtype)

    if lax.axis_size("col") != 4:
        return total(parts)
    return jnp.concatenate([total(parts[:3]), total(parts[3:])])


def place(row, col, n_col):
    return row * n_col + col


def spread_start(block):
    n_col = lax.axis_size("col")
    n_row = lax.axis_size("row")
    deep = n_row // n_col
    pieces = []
    for low in range(deep):
        for step in range(n_col):
            pairs = []
            for to_row in range(n_row):
                for to_col in range(n_col):
                    from_row = to_col * deep + ((to_row % deep) ^ low)
                    from_col = (to_row // deep) ^ step
                    pairs.append(
                        (place(from_row, from_col, n_col), place(to_row, to_col, n_col))
                    )
            pieces.append(lax.ppermute(block, ("row", "col"), pairs))
    return pieces


def spread_finish(pieces):
    n_col = lax.axis_size("col")
    deep = lax.axis_size("row") // n_col
    row = lax.axis_index("row")
    tokens, width = pieces[0].shape
    wide = jnp.zeros((deep * tokens, n_col * width), pieces[0].dtype)
    offset = (row // deep) ^ lax.axis_index("col")
    for number, piece in enumerate(pieces):
        at_row = ((row % deep) ^ (number // n_col)) * tokens
        at_col = (offset ^ (number % n_col)) * width
        wide = lax.dynamic_update_slice(wide, piece, (at_row, at_col))
    return wide


def dp_parts(own):
    return [own] + [swap(own, "dp", step) for step in range(1, lax.axis_size("dp"))]


def collect_first(partial):
    n_dp = lax.axis_size("dp")
    tokens = partial.shape[0] // n_dp
    summed = partial[:tokens]
    for step in range(1, n_dp):
        other = swap(partial[step * tokens : (step + 1) * tokens], "dp", step)
        summed = add_wide(summed, other)
    return summed


def collect_second(summed):
    n_col = lax.axis_size("col")
    col = lax.axis_index("col")
    tokens = summed.shape[0]
    width = summed.shape[1] // n_col
    groups = jnp.zeros((n_col, tokens, width), summed.dtype)
    for step in range(n_col):
        piece = summed[:, step * width : (step + 1) * width]
        if step:
            piece = swap(piece, "col", step)
        groups = lax.dynamic_update_slice(groups, piece[None], (col ^ step, 0, 0))
    return groups


def collect_third(groups):
    n_row = lax.axis_size("row")
    row = lax.axis_index("row")
    blocks = groups.reshape(n_row, -1, groups.shape[-1])
    take = lambda step: lax.dynamic_index_in_dim(blocks, row ^ step, 0, keepdims=False)
    held = {step: take(step) for step in range(n_row)}
    bit = 1
    while bit < n_row:
        sent = jnp.stack([held[step] for step in sorted(held) if step & bit])
        got = swap(sent, "row", bit)
        kept = [step for step in sorted(held) if not step & bit]
        last = 2 * bit >= n_row
        held = {
            step: held[step].astype(jnp.float32) + got[place].astype(jnp.float32)
            for place, step in enumerate(kept)
        }
        if not last:
            held = {step: value.astype(groups.dtype) for step, value in held.items()}
        bit *= 2
    return held[0].astype(jnp.float32)


def late_kernel(*refs):
    out_ref = refs[-1]
    count = len(refs) // 4
    split = refs[count].shape[1]

    def total(lefts, rights):
        out = dot_tn(lefts[0][...], rights[0][...])
        for left, right in zip(lefts[1:], rights[1:]):
            out = out + dot_tn(left[...], right[...])
        return out.astype(jnp.bfloat16)

    out_ref[:, :split] = total(refs[:count], refs[count : 2 * count])
    out_ref[:, split:] = total(refs[2 * count : 3 * count], refs[3 * count : 4 * count])


def late_grads(normed_parts, grad_qkv, grad_parts, attended):
    tokens, full = normed_parts[0].shape
    count = len(normed_parts)
    columns = grad_qkv.shape[1] + attended.shape[1]
    tile = 512
    left = [pl.BlockSpec((tokens, tile), lambda i: (0, i))] * count
    right = lambda array: [
        pl.BlockSpec((tokens, array.shape[1]), lambda i, part=part: (part, 0))
        for part in range(count)
    ]
    return pl.pallas_call(
        late_kernel,
        grid=(full // tile,),
        in_specs=left + right(grad_qkv) + left + right(attended),
        out_specs=pl.BlockSpec((tile, columns), lambda i: (i, 0)),
        out_shape=jax.ShapeDtypeStruct((full, columns), jnp.bfloat16),
    )(*normed_parts, *[grad_qkv] * count, *grad_parts, *[attended] * count)


def half_of(array, axis):
    size = array.shape[axis] // lax.axis_size("dp")
    return lax.dynamic_slice_in_dim(array, lax.axis_index("dp") * size, size, axis)


def both_halves(own, axis):
    n_dp = lax.axis_size("dp")
    here = lax.axis_index("dp")
    parts = [own] + [swap(own, "dp", step) for step in range(1, n_dp)]
    if n_dp == 2:
        low = jnp.where(here == 0, parts[0], parts[1])
        high = jnp.where(here == 0, parts[1], parts[0])
        return jnp.concatenate([low, high], axis=axis)
    size = own.shape[axis]
    out = jnp.concatenate(parts, axis=axis)
    for step in range(n_dp):
        out = lax.dynamic_update_slice_in_dim(out, parts[step], (here ^ step) * size, axis)
    return out


def body(
    inputs,
    segment,
    grad_output,
    norm_gain,
    norm_bias,
    qkv_weight,
    qkv_bias,
    dense_weight,
    dense_bias,
    fc1_weight,
    fc1_bias,
    fc2_weight,
    fc2_bias,
):
    n_col = lax.axis_size("col")
    n_dp = lax.axis_size("dp")
    width = inputs.shape[1]
    full_width = n_col * width
    qkv_cols = qkv_weight.shape[1] // n_dp
    att_cols = dense_weight.shape[0] // n_dp
    wide_in = inputs.astype(jnp.float32)
    own_sums = jnp.stack([jnp.sum(wide_in, axis=1), jnp.sum(wide_in * wide_in, axis=1)])
    scales = jnp.stack([norm_gain, norm_bias])
    scales = jnp.concatenate(
        [scales]
        + [swap(scales, "col", step) for step in range(1, n_col)],
        axis=1,
    )
    in_pieces = spread_start(inputs)
    fc1_blocks, fc1_early = grid_gather(half_of(fc1_weight, 1))
    grad_pieces = spread_start(grad_output)
    back_half = jnp.concatenate([half_of(dense_weight, 0), half_of(fc2_weight, 0)], axis=0)
    back_blocks, back_early = grid_gather(after(back_half, *fc1_early))
    qkv_blocks, _ = grid_gather(after(half_of(qkv_weight, 1), *back_early))
    fc1_all = jnp.concatenate(fc1_blocks)
    back_all = jnp.concatenate(back_blocks, axis=1)
    qkv_all = jnp.concatenate(qkv_blocks)
    seg_rows = jnp.concatenate(dp_parts(segment))
    cosines, sines = rotary_tables(seg_rows, qkv_cols)

    def centre(wide_in, row_total, row_squares):
        row_mean = (row_total / full_width)[:, None]
        row_square = (row_squares / full_width)[:, None]
        inv_std = lax.rsqrt(row_square - row_mean * row_mean + EPS)
        return (wide_in - row_mean) * inv_std, inv_std

    in_pieces = list(
        lax.optimization_barrier(tuple(in_pieces) + (cosines, sines))[:-2]
    )
    wide_rows = spread_finish(in_pieces).astype(jnp.float32)
    centered_rows, _ = centre(
        wide_rows, jnp.sum(wide_rows, axis=1), jnp.sum(wide_rows * wide_rows, axis=1)
    )
    normed_own = (centered_rows * scales[:1] + scales[1:]).astype(jnp.bfloat16)
    normed_parts = dp_parts(normed_own)
    normed_rows = jnp.concatenate(normed_parts)

    fc1_shift = half_of(fc1_bias, 0)
    pre_act = dot_nn(normed_rows, fc1_all) + fc1_shift
    hidden = gelu_tanh(pre_act).astype(jnp.bfloat16)
    grad_pieces = list(lax.optimization_barrier(tuple(grad_pieces) + (normed_own,))[:-1])
    grad_parts = dp_parts(spread_finish(grad_pieces))
    grad_rows = jnp.concatenate(grad_parts)
    fc2_part = dot_tn(grad_rows, hidden).astype(jnp.bfloat16)
    fc2_kept, fc2_got = scatter_first(fc2_part)

    backed = dot_nt(after(grad_rows, fc2_part), back_all)
    grad_att = backed[:, :att_cols].astype(jnp.bfloat16)
    grad_pre = (backed[:, att_cols:] * gelu_slope(pre_act)).astype(jnp.bfloat16)
    fc1_part = dot_tn(normed_rows, grad_pre).astype(jnp.bfloat16)
    fc1_kept, fc1_got = scatter_first(fc1_part)

    attended, grad_qkv = attention(
        after(dot_nn(normed_rows, qkv_all), fc1_part),
        half_of(qkv_bias, 0),
        cosines,
        sines,
        seg_rows,
        grad_att,
    )
    bias_sums = jnp.concatenate(
        [
            jnp.sum(grad_qkv.astype(jnp.float32), axis=0, keepdims=True),
            jnp.sum(grad_pre.astype(jnp.float32), axis=0, keepdims=True),
        ],
        axis=1,
    )
    fc2_got = list(lax.optimization_barrier((tuple(fc2_got), grad_qkv))[0])
    fc2_sent, fc2_parts = scatter_second(fc2_kept, fc2_got)
    fc1_got = list(lax.optimization_barrier((tuple(fc1_got), grad_qkv))[0])
    fc1_sent, fc1_parts = scatter_second(fc1_kept, fc1_got)
    norm_part = (
        dot_nt(after(grad_qkv, *fc2_sent), qkv_all) + dot_nt(after(grad_pre, fc1_part), fc1_all)
    ).astype(jnp.bfloat16)
    norm_summed = collect_first(norm_part)
    acts = after(jnp.concatenate([attended, hidden], axis=1), norm_summed, *fc1_sent)
    mixed_part = dot_nn(acts, back_all).astype(jnp.bfloat16)
    mixed_summed = after(collect_first(mixed_part), norm_summed)
    norm_groups = collect_second(norm_summed)
    mixed_groups = collect_second(mixed_summed)

    late_part = late_grads(
        normed_parts, after(grad_qkv, mixed_summed), grad_parts, attended
    )
    late_kept, late_got = scatter_first(late_part)
    grad_normed = collect_third(norm_groups)
    mixed_groups = after(mixed_groups, norm_groups)
    mixed = collect_third(mixed_groups)
    late_got = list(lax.optimization_barrier((tuple(late_got), mixed_groups))[0])
    late_sent, late_parts = scatter_second(late_kept, late_got)

    fc2_parts = lax.optimization_barrier((tuple(fc2_parts), tuple(late_sent)))[0]
    grad_fc2_t = scatter_last(list(fc2_parts))
    fc1_parts = lax.optimization_barrier((tuple(fc1_parts), grad_fc2_t))[0]
    grad_fc1 = scatter_last(list(fc1_parts))
    wide = lambda array: array.astype(jnp.float32)
    out_fc1 = wide(both_halves(grad_fc1, 1))
    out_fc2 = wide(both_halves(grad_fc2_t.T, 0))
    grad_normed = after(grad_normed, out_fc1, out_fc2, *late_sent)
    late_parts = lax.optimization_barrier((tuple(late_parts), grad_normed))[0]
    late_qkv = scatter_last([part[:, :qkv_cols] for part in late_parts])
    late_dense = scatter_last([part[:, qkv_cols:] for part in late_parts])

    grad_in_b = total_over(bias_sums, ("col",), norm_groups, grad_fc1)
    sums = total_over(own_sums, ("col",), scales, late_part)
    centered, inv_std = centre(wide_in, sums[0], sums[1])
    scaled = grad_normed * norm_gain
    cross = total_over(
        jnp.stack([jnp.sum(scaled, axis=1), jnp.sum(scaled * centered, axis=1)]), ("col",)
    )
    grad_wide = grad_output.astype(jnp.float32)
    grad_input = grad_wide + inv_std * (
        scaled - (cross[0] / full_width)[:, None] - centered * (cross[1] / full_width)[:, None]
    )
    own_norm = jnp.stack(
        [
            jnp.sum(grad_normed * centered, axis=0),
            jnp.sum(grad_normed, axis=0),
            jnp.sum(grad_wide, axis=0),
        ]
    )
    norm_sums = total_over(own_norm, ("dp", "row"))
    mixed = after(mixed, own_norm)
    output = (wide_in + (mixed + dense_bias + fc2_bias)).astype(jnp.bfloat16)
    return (
        output,
        grad_input,
        norm_sums[0],
        norm_sums[1],
        wide(both_halves(late_qkv, 1)),
        both_halves(grad_in_b[0, :qkv_cols], 0),
        wide(both_halves(late_dense.T, 0)),
        norm_sums[2],
        out_fc1,
        both_halves(grad_in_b[0, qkv_cols:], 0),
        out_fc2,
        norm_sums[2],
    )


def solution(mesh):
    in_specs = (
        P(("dp", "row"), "col"),
        P(("dp", "col"), None),
        P(("dp", "row"), "col"),
        P("col"),
        P("col"),
        P("col", "row"),
        P("row"),
        P("row", "col"),
        P("col"),
        P("col", "row"),
        P("row"),
        P("row", "col"),
        P("col"),
    )
    out_specs = (
        P(("dp", "row"), "col"),
        P(("dp", "row"), "col"),
        P("col"),
        P("col"),
        P("col", "row"),
        P("row"),
        P("row", "col"),
        P("col"),
        P("col", "row"),
        P("row"),
        P("row", "col"),
        P("col"),
    )

    return jax.shard_map(body, mesh=mesh, in_specs=in_specs, out_specs=out_specs, check_vma=False)
```
